128 devices in a mesh: grp: 4 (over z), list: 32 (over y, x, core).
Axes of the slice: x: 4, y: 4, z: 4, core: 2. Of those that a mesh axis runs over, the one named last changes fastest.
Arguments:
- vectors: bfloat16 [3, 65536, 1024], P(None, ('grp', 'list')), may hold values from -6 to 6
- owner_route: int32 [3, 65536, 1], P(None, ('grp', 'list')), may hold values from 0 to 31; in each aligned block of 512 rows (0 to 511, 512 to 1023, ..., all dimensions but the last counted through in order) at most 32 rows name the same one
- list_slot: int32 [3, 65536], P(None, ('grp', 'list')), may hold values from 0 to 1023
- centroids: float32 [32768, 1024], P('list'), may hold values from -6 to 6
- counts: int32 [32768], P('list'), may hold values from 1 to 8
Outputs:
- residuals: bfloat16 [3, 65536, 1024], P(None, ('grp', 'list'))
- new_centroids: float32 [32768, 1024], P('list')
The draws below stay inside these ranges and needn't reach their ends.
Inputs may be any that keep to these rules, and one draw needn't show every extreme that they name: `owner_route`: within the rows of one device for one step, at most 32 vectors name the same owner; some owner is named exactly 32 times.
All inputs are finite; a program needn't handle non-finite values.
Results may differ from the reference program's by a relative error of at most 0.0035.
Values may be sent and summed in bfloat16 or wider, within the bound.
No kernel may reach another device: no remote copies, remote signals or barrier semaphores. Data moves between devices by JAX's collectives and lax.ppermute only.
A program may use at most 128 MiB of HBM per device.

```python
import math
import jax
import jax.numpy as jnp
import numpy as np

D = 1024
LIST_DEV = 1024
ROWS = 512
STEPS = 3
OWNERS = 32
CAP = 32
LISTS = 32768
VECS = 65536


def set_ends(entries, key, smallest, largest):
    index_at = [jax.random.randint(jax.random.fold_in(key, axis), (), 0, length) for axis, length in enumerate(entries.shape)]
    widest = entries.shape.index(max(entries.shape))
    next_to = index_at[:widest] + [(index_at[widest] + 1) % entries.shape[widest]] + index_at[widest + 1:]
    return entries.at[tuple(index_at)].set(smallest).at[tuple(next_to)].set(largest)


def steps_of(stream_key, extent, shards, low, largest):
    loudness = 1.0
    for dim, blocks in shards:
        draws = jax.random.uniform(jax.random.fold_in(jax.random.fold_in(stream_key, 6), dim), (blocks,), jnp.float32, low / len(shards), largest / len(shards))
        loudness = loudness * jnp.repeat(jnp.exp(draws), extent[dim] // blocks).reshape((-1,) + (1,) * (len(extent) - 1 - dim))
    return loudness


def deal_out(key, own, number, rows, number_of, top, most, lean):
    sequence = jax.random.permutation(key, number_of)
    crowded, ordinary = shares(number_of, rows * top, most, lean, True), shares(number_of, rows * top, most, lean, False)
    places = jnp.arange(number_of)

    def named(tallies, turn):
        used = int((tallies > 0).sum())
        fixed = max(1, used // 4)
        shifted = fixed + (places - fixed + turn * (used - fixed)) % max(1, number_of - fixed)
        return jnp.zeros((number_of,), jnp.int32).at[sequence[jnp.where(places < fixed, places, shifted)]].set(jnp.asarray(tallies, jnp.int32))

    tallies = jnp.where(number % 4 == 0, named(crowded, number // 4), named(ordinary, number - number // 4 - 1))
    mixed = jax.random.permutation(jax.random.fold_in(own, 3), number_of)
    giver, sink = mixed[0:number_of // 2 * 2:2], mixed[1:number_of // 2 * 2:2]
    room = jnp.minimum(tallies[giver] - 1, most - tallies[sink]) // 2
    room = jnp.where((giver == sequence[0]) | (sink == sequence[0]) | (tallies[sink] == 0), 0, jnp.maximum(room, 0))
    shifted = jax.random.randint(jax.random.fold_in(own, 4), (number_of // 2,), 0, 1 << 20) % (room + 1)
    tallies = tallies.at[giver].add(-shifted).at[sink].add(shifted)
    items = jnp.searchsorted(jnp.cumsum(tallies), jnp.arange(rows * top), side="right").astype(jnp.int32)
    listing = items.reshape(top, rows).T
    listing = listing[jax.random.permutation(jax.random.fold_in(own, 1), rows)]
    turn = jax.random.randint(jax.random.fold_in(own, 2), (rows, 1), 0, top)
    return jnp.take_along_axis(listing, (jnp.arange(top)[None, :] + turn) % top, axis=1)


def shares(amount, total, bound, lean, full):
    portions = [(1 << 20) // math.isqrt(standing ** lean) + 1 for standing in range(1, amount + 1)]
    largest = bound if full else min(bound, max(-(-total // amount), total * portions[0] // sum(portions)))
    least = 1 if total - largest >= amount - 1 else 0
    given, surplus = [largest] + [least] * (amount - 1), total - largest - least * (amount - 1)
    while surplus > 0:
        candidates = [i for i in range(1, amount) if given[i] < largest] or [i for i in range(1, amount) if given[i] < bound]
        whole, remaining = sum([portions[i] for i in candidates]), surplus
        for i in candidates:
            more = min(bound - given[i], max(1, remaining * portions[i] // whole), surplus)
            given[i] = given[i] + more
            surplus = surplus - more
    return np.array(given)


def bell_draw(rng, dims, spread, limit, split=(), held_as=jnp.bfloat16):
    array = jax.random.normal(rng, dims, jnp.float32) * spread
    if len(split) > 0:
        array = steps_of(rng, dims, split, -0.22, 0.18) * array
    return jnp.clip(array, min=-limit, max=limit).astype(held_as)


def setup_inputs(seed: int = 0) -> dict:
    streams_of = jax.random.split(jax.random.key(seed), 6)
    vectors = bell_draw(streams_of[0], (STEPS, VECS, D), 1.0, 6.0, ((1, 128),))
    owner_route_keys = jax.random.split(jax.random.fold_in(streams_of[1], 1), STEPS * VECS // ROWS)
    owner_route_turns = jax.random.permutation(jax.random.fold_in(streams_of[1], 3), STEPS * VECS // ROWS)
    owner_route = jax.vmap(lambda own, number: deal_out(jax.random.fold_in(streams_of[1], 2), own, number, ROWS, OWNERS, 1, CAP, 2))(owner_route_keys, owner_route_turns).reshape((STEPS, VECS, 1))
    list_slot = set_ends(jax.random.randint(streams_of[2], (STEPS, VECS), 0, LIST_DEV), jax.random.fold_in(streams_of[2], 1), 0, LIST_DEV - 1).astype(jnp.int32)
    centroids = bell_draw(streams_of[3], (LISTS, D), 1.0, 6.0, ((0, 32),), jnp.float32)
    counts = set_ends(jax.random.randint(streams_of[4], (LISTS,), 1, 9), jax.random.fold_in(streams_of[4], 1), 1, 8).astype(jnp.int32)
    return {"vectors": vectors, "owner_route": owner_route, "list_slot": list_slot, "centroids": centroids, "counts": counts}


def reference(vectors, owner_route, list_slot, centroids, counts):
    current = centroids
    weights = counts.astype(jnp.float32)
    outputs = []
    for step_index in range(STEPS):
        list_ids = (owner_route[step_index, :, 0] * LIST_DEV + list_slot[step_index]).astype(jnp.int32)
        vec_float = vectors[step_index].astype(jnp.float32)
        residual_rows = (vec_float - current[list_ids]).astype(jnp.bfloat16)
        outputs.append(residual_rows)
        sums = jax.ops.segment_sum(vec_float, list_ids, num_segments=LISTS)
        batch_count = jax.ops.segment_sum(jnp.ones((vec_float.shape[0],), jnp.float32), list_ids, num_segments=LISTS)
        current = (weights[:, None] * current + sums) / (weights + batch_count)[:, None]
        weights = weights + batch_count
    return jnp.stack(outputs, axis=0), current
```

```python
import jax
import jax.numpy as jnp
from jax import lax
from jax.sharding import PartitionSpec as P

STEPS = 3


def tie(value, *others):
    return lax.optimization_barrier((value,) + others)[0]


def split_table(table):
    hi = lax.reduce_precision(table, 8, 7)
    lo = table - hi
    return jnp.concatenate([hi.astype(jnp.bfloat16), lo.astype(jnp.bfloat16)], axis=0)


def local(vectors, owner_route, list_slot, centroids, counts):
    owner_count = lax.axis_size("list")
    grp_count = lax.axis_size("grp")
    row_count = vectors.shape[1]
    width = vectors.shape[2]
    capacity = 2 * row_count // owner_count
    list_dev = centroids.shape[0]
    total_rows = owner_count * capacity

    owner_ids = owner_route[:, :, 0]
    hits = owner_ids[:, :, None] == jnp.arange(owner_count, dtype=jnp.int32)
    earlier = jnp.arange(row_count)[:, None] > jnp.arange(row_count)[None, :]
    before = jnp.einsum(
        "ij,sjo->sio",
        earlier.astype(jnp.bfloat16),
        hits.astype(jnp.bfloat16),
        preferred_element_type=jnp.float32,
    )
    rank = jnp.sum(jnp.where(hits, before, 0.0), axis=2).astype(jnp.int32)
    dest = owner_ids * capacity + rank

    row_iota = jnp.arange(total_rows, dtype=jnp.int32)
    place = dest[:, None, :] == row_iota[None, :, None]
    slots = jnp.sum(jnp.where(place, list_slot[:, None, :] + 1, 0), axis=2) - 1
    slots = slots.reshape(STEPS, owner_count, capacity).transpose(1, 0, 2)
    slots = slots.reshape(owner_count, 1, STEPS * capacity)
    slots = lax.all_to_all(slots, "list", split_axis=0, concat_axis=0, tiled=True)
    slots = slots.reshape(owner_count, STEPS, capacity).transpose(1, 0, 2)
    slots = slots.reshape(STEPS, total_rows)

    list_iota = jnp.arange(list_dev, dtype=jnp.int32)
    batch = jnp.sum((slots[:, None, :] == list_iota[None, :, None]).astype(jnp.int32), axis=2)
    parts = [batch]
    for offset in range(1, grp_count):
        parts.append(
            lax.ppermute(batch, "grp", [(i, (i + offset) % grp_count) for i in range(grp_count)])
        )
    batch = sum(parts).astype(jnp.float32)

    def exchange(rows):
        rows = rows.reshape(owner_count, capacity, width)
        rows = lax.all_to_all(rows, "list", split_axis=0, concat_axis=0, tiled=True)
        return rows.reshape(total_rows, width)

    received = []
    for step in range(STEPS):
        send = jnp.dot(
            (dest[step][None, :] == row_iota[:, None]).astype(jnp.bfloat16),
            vectors[step],
            preferred_element_type=jnp.float32,
        ).astype(jnp.bfloat16)
        if received:
            send = tie(send, received[-1])
        received.append(exchange(send))

    totals = []
    for step in range(STEPS):
        one_hot = (list_iota[:, None] == slots[step][None, :]).astype(jnp.bfloat16)
        sums = jnp.dot(one_hot, received[step], preferred_element_type=jnp.float32)
        sums = sums.astype(jnp.bfloat16)
        if totals:
            sums = tie(sums, totals[-1])
        totals.append(lax.psum(sums, "grp"))

    weights = counts.astype(jnp.float32)
    mass = weights[:, None] * centroids
    current = centroids
    outputs = []
    last = received[-1]
    backs = []
    for step in range(STEPS):
        one_hot = slots[step][:, None] == (jnp.arange(2 * list_dev, dtype=jnp.int32) % list_dev)[None, :]
        chosen = jnp.dot(
            one_hot.astype(jnp.bfloat16), split_table(current), preferred_element_type=jnp.float32
        )
        residual = (received[step].astype(jnp.float32) - chosen).astype(jnp.bfloat16)
        back = exchange(tie(residual, last))
        last = back
        backs.append(back)
        pick = (dest[step][:, None] == row_iota[None, :]).astype(jnp.bfloat16)
        outputs.append(jnp.dot(pick, back, preferred_element_type=jnp.float32).astype(jnp.bfloat16))
        total = tie(totals[step], received[-1] if step == 0 else backs[-2])
        mass = mass + total.astype(jnp.float32)
        weights = weights + batch[step]
        current = mass / weights[:, None]
    return (jnp.stack(outputs, axis=0), current)


def solution(mesh):
    in_specs = (
        P(None, ("grp", "list"), None),
        P(None, ("grp", "list"), None),
        P(None, ("grp", "list")),
        P("list", None),
        P("list"),
    )
    out_specs = (P(None, ("grp", "list"), None), P("list", None))
    return jax.shard_map(local, mesh=mesh, in_specs=in_specs, out_specs=out_specs, check_vma=False)
```

```python
import jax
import jax.numpy as jnp
from jax import lax
from jax.experimental import pallas as pl
from jax.experimental.pallas import tpu as pltpu
from jax.sharding import PartitionSpec as P

STEPS = 3
BLOCK = 512
CHEAP = pl.CostEstimate(flops=1, bytes_accessed=1, transcendentals=0)


def gate(*values):
    return lax.optimization_barrier(values)


def swap(rows, axis, offset):
    count = lax.axis_size(axis)
    return lax.ppermute(rows, axis, [(i, i ^ offset) for i in range(count)])


def select(hit):
    return jnp.where(hit, 1.0, 0.0).astype(jnp.bfloat16)


def mix(left, right):
    return jnp.dot(left, right, preferred_element_type=jnp.float32)


def pack_rows(vectors, dest, step, owners, capacity, count):
    row_count, width = vectors.shape[1:]
    group = BLOCK // capacity

    def body(dest_ref, vec_ref, out_ref):
        rows = lax.broadcasted_iota(jnp.int32, (BLOCK, row_count), 0) + pl.program_id(0) * BLOCK
        picked = mix(select(rows == dest_ref[0]), vec_ref[0]).astype(jnp.bfloat16)
        out_ref[...] = picked.reshape(group, 1, capacity, width)

    return pl.pallas_call(
        body,
        grid=(owners // group,),
        in_specs=[
            pl.BlockSpec((1, 1, row_count), lambda b: (step, 0, 0)),
            pl.BlockSpec((1, row_count, width), lambda b: (step, 0, 0)),
        ],
        out_specs=pl.BlockSpec((group, 1, capacity, width), lambda b: (b, 0, 0, 0)),
        out_shape=jax.ShapeDtypeStruct((owners, count, capacity, width), jnp.bfloat16),
        name="pack_rows",
        cost_estimate=CHEAP,
    )(dest, vectors)


def list_sums(received, at, slots, step, list_dev):
    owners, _, capacity, width = received.shape
    rows = owners * capacity
    sizes = [list_dev // 8, list_dev // 8, list_dev // 4] * 2

    def body(slot_ref, row_ref, *outs):
        data = row_ref[...].reshape(rows, width)
        first = 0
        for half in range(2):
            lists = lax.broadcasted_iota(jnp.int32, (list_dev // 2, rows), 0) + first
            sums = mix(select(lists == slot_ref[0]), data).astype(jnp.bfloat16)
            at = 0
            for out_ref in outs[3 * half : 3 * half + 3]:
                out_ref[...] = sums[at : at + out_ref.shape[0]]
                at += out_ref.shape[0]
            first += list_dev // 2

    return pl.pallas_call(
        body,
        grid=(1,),
        in_specs=[
            pl.BlockSpec((1, 1, rows), lambda i: (step, 0, 0)),
            pl.BlockSpec((owners, 1, capacity, width), lambda i: (0, at, 0, 0)),
        ],
        out_specs=[pl.BlockSpec((size, width), lambda i: (0, 0)) for size in sizes],
        out_shape=[jax.ShapeDtypeStruct((size, width), jnp.bfloat16) for size in sizes],
        name="list_sums",
        cost_estimate=CHEAP,
    )(slots, received)


def update(step, index, place_ref, weight_ref, table_ref, parts, store):
    chunk = table_ref.shape[0]
    slab = 16

    def run(piece, base):
        def one(k, carry):
            at = pl.ds(pl.multiple_of(k * slab, slab), slab)
            table = table_ref[at, :]
            if parts:
                away = pl.ds(pl.multiple_of(base + k * slab, slab), slab)
                total = parts[0][piece][away, :].astype(jnp.float32)
                for four in parts[1:]:
                    total = total + four[piece][away, :].astype(jnp.float32)
                weights = weight_ref[at, :]
                share = 1.0 / weights[:, step : step + 1]
                table = (weights[:, :1] * table + total) * share
            store(index * chunk + k * slab, at, table)
            return carry

        lax.fori_loop(0, chunk // slab, one, 0, unroll=4)

    if not parts:
        run(0, 0)
        return
    half = index // 4
    relative = (index % 4) ^ place_ref[half]
    mine = 2 * half + relative // 2
    for piece in range(4):
        pl.when(mine == piece)(lambda piece=piece: run(piece, (relative % 2) * chunk))


def part_specs(parts):
    return [pl.BlockSpec(p.shape, lambda i, group: (0, 0)) for four in parts for p in four]


def fours(refs):
    return [refs[k : k + 4] for k in range(0, len(refs), 4)]


def residual_rows(received, at, slots, step, centroids, weights, parts, places, into, place, count):
    owners, _, capacity, width = received.shape
    list_dev = centroids.shape[0]
    group = BLOCK // capacity
    blocks = owners // group
    chunks = 8
    chunk = list_dev // chunks
    part_count = 4 * len(parts)

    def body(place_ref, slot_ref, row_ref, table_ref, weight_ref, *rest):
        out_ref, pair_ref = rest[-2:]
        index = pl.program_id(0)

        def store(first, at, table):
            hi = table.astype(jnp.bfloat16)
            lo = (table - hi.astype(jnp.float32)).astype(jnp.bfloat16)
            pair_ref[pl.ds(pl.multiple_of(first, 16), 16), :] = hi
            pair_ref[pl.ds(pl.multiple_of(list_dev + first, 16), 16), :] = lo

        @pl.when(index < chunks)
        def _():
            update(step, index, place_ref, weight_ref, table_ref, fours(rest[:part_count]), store)

        @pl.when(index >= chunks)
        def _():
            lists = lax.broadcasted_iota(jnp.int32, (BLOCK, list_dev), 1)
            hit = select(lists == slot_ref[:, step : step + 1])
            chosen = mix(jnp.concatenate([hit, hit], axis=1), pair_ref[...])
            data = row_ref[...].reshape(BLOCK, width).astype(jnp.float32)
            out_ref[...] = (data - chosen).astype(jnp.bfloat16).reshape(group, 1, capacity, width)

    def late(i):
        return jnp.maximum(i - chunks, 0)

    def early(i):
        return jnp.minimum(i, chunks - 1)

    in_specs = [
        pl.BlockSpec((BLOCK, STEPS), lambda i, places: (late(i), 0)),
        pl.BlockSpec((group, 1, capacity, width), lambda i, places: (late(i), at, 0, 0)),
        pl.BlockSpec((chunk, width), lambda i, places: (early(i), 0)),
        pl.BlockSpec((chunk, STEPS + 1), lambda i, places: (early(i), 0)),
    ] + part_specs(parts)
    args = [slots, received, centroids, weights] + [p for four in parts for p in four]
    aliases = {}
    if into is not None:
        in_specs.append(pl.BlockSpec(memory_space=pl.ANY))
        aliases = {1 + len(args): 0}
        args.append(into)
    return pl.pallas_call(
        body,
        grid_spec=pltpu.PrefetchScalarGridSpec(
            num_scalar_prefetch=1,
            grid=(chunks + blocks,),
            in_specs=in_specs,
            out_specs=pl.BlockSpec(
                (group, 1, capacity, width), lambda i, places: (late(i), place, 0, 0)
            ),
            scratch_shapes=[pltpu.VMEM((2 * list_dev, width), jnp.bfloat16)],
        ),
        out_shape=jax.ShapeDtypeStruct((owners, count, capacity, width), jnp.bfloat16),
        input_output_aliases=aliases,
        name="residual_rows",
        cost_estimate=CHEAP,
    )(places, *args)


def new_rows(centroids, weights, parts, places):
    list_dev, width = centroids.shape
    chunk = list_dev // 8

    def body(place_ref, table_ref, weight_ref, *rest):
        def store(first, at, table):
            rest[-1][at, :] = table

        update(STEPS, pl.program_id(0), place_ref, weight_ref, table_ref, fours(rest[:-1]), store)

    return pl.pallas_call(
        body,
        grid_spec=pltpu.PrefetchScalarGridSpec(
            num_scalar_prefetch=1,
            grid=(8,),
            in_specs=[
                pl.BlockSpec((chunk, width), lambda i, places: (i, 0)),
                pl.BlockSpec((chunk, STEPS + 1), lambda i, places: (i, 0)),
            ]
            + part_specs(parts),
            out_specs=pl.BlockSpec((chunk, width), lambda i, places: (i, 0)),
        ),
        out_shape=jax.ShapeDtypeStruct((list_dev, width), jnp.float32),
        name="new_rows",
        cost_estimate=CHEAP,
    )(places, centroids, weights, *[p for four in parts for p in four])


def unpack_rows(back, at, dest, step, into, row_count):
    owners, _, capacity, width = back.shape
    rows = owners * capacity

    def body(dest_ref, row_ref, *rest):
        places = lax.broadcasted_iota(jnp.int32, (row_count, rows), 1)
        data = row_ref[...].reshape(rows, width)
        hit = select(places == dest_ref[:, step : step + 1])
        rest[-1][0] = mix(hit, data).astype(jnp.bfloat16)

    in_specs = [
        pl.BlockSpec((row_count, STEPS), lambda b: (0, 0)),
        pl.BlockSpec((owners, 1, capacity, width), lambda b: (0, at, 0, 0)),
    ]
    args = [dest, back]
    aliases = {}
    if into is not None:
        in_specs.append(pl.BlockSpec(memory_space=pl.ANY))
        args.append(into)
        aliases = {2: 0}
    return pl.pallas_call(
        body,
        grid=(1,),
        in_specs=in_specs,
        out_specs=pl.BlockSpec((1, row_count, width), lambda b: (step, 0, 0)),
        out_shape=jax.ShapeDtypeStruct((STEPS, row_count, width), jnp.bfloat16),
        input_output_aliases=aliases,
        name="unpack_rows",
        cost_estimate=CHEAP,
    )(*args)


def add(*values):
    total = values[0].astype(jnp.float32)
    for value in values[1:]:
        total = total + value.astype(jnp.float32)
    return total.astype(jnp.bfloat16)


def scatter_sum(parts):
    got = [swap(parts[2], "grp", 1), swap(parts[5], "grp", 3)]
    block = parts[0].shape[0]
    over = [swap(add(parts[3 * h + 1], got[h][block:]), "grp", 3 - 2 * h) for h in range(2)]
    return [add(parts[3 * h], got[h][:block], over[h]) for h in range(2)]


def gather_sum(done):
    own = [jnp.concatenate([done[h], swap(done[h], "grp", 3 - 2 * h)]) for h in range(2)]
    near = [swap(own[h], "grp", 1 + 2 * h) for h in range(2)]
    return [own[0], near[0], own[1], near[1]]


def exchange(rows):
    return lax.all_to_all(rows, "list", split_axis=0, concat_axis=0, tiled=True)


def local(vectors, owner_route, list_slot, centroids, counts):
    owners = lax.axis_size("list")
    grp_count = lax.axis_size("grp")
    row_count = vectors.shape[1]
    capacity = 2 * row_count // owners
    list_dev = centroids.shape[0]
    group = lax.axis_index("grp")
    assert grp_count == 4

    owner_ids = owner_route[:, :, 0]
    hits = owner_ids[:, None, :] == jnp.arange(owners, dtype=jnp.int32)[None, :, None]
    earlier = jnp.arange(row_count)[:, None] < jnp.arange(row_count)[None, :]
    rank = mix(
        hits.reshape(STEPS * owners, row_count).astype(jnp.bfloat16), earlier.astype(jnp.bfloat16)
    )
    rank = jnp.sum(jnp.where(hits, rank.reshape(hits.shape), 0.0), axis=1).astype(jnp.int32)
    dest = owner_ids * capacity + rank
    dest_lanes = dest.reshape(STEPS, 1, row_count)

    places = jnp.arange(owners * capacity, dtype=jnp.int32)
    found = dest[:, None, :] == places[None, :, None]
    slots = jnp.sum(jnp.where(found, list_slot[:, None, :] + 1, 0), axis=2) - 1
    slots = slots.reshape(STEPS, owners, capacity).transpose(1, 0, 2)
    slots = exchange(slots.reshape(owners, 1, STEPS * capacity))

    first = pack_rows(vectors, dest_lanes, 0, owners, capacity, 1)
    first, slots = gate(first, slots)
    received0 = exchange(first)
    second = pack_rows(vectors, dest_lanes, 1, owners, capacity, 1)
    third = pack_rows(vectors, dest_lanes, 2, owners, capacity, 2)

    slots = slots.reshape(owners, STEPS, capacity).transpose(1, 0, 2)
    slots = slots.reshape(STEPS, owners * capacity)
    slot_cols = slots.T
    dest_cols = dest.T

    list_iota = jnp.arange(list_dev, dtype=jnp.int32)
    batch = jnp.sum((slots[:, None, :] == list_iota[None, :, None]).astype(jnp.int32), axis=2)
    batch = sum([batch] + [swap(batch, "grp", offset) for offset in range(1, grp_count)])
    weights = [counts]
    for step in range(STEPS):
        weights.append(weights[-1] + batch[step])
    weights = jnp.stack(weights).astype(jnp.float32).T

    high = group // 2
    low = (group ^ high) % 2
    places = jnp.stack([2 * low + high, 2 * high + low]).astype(jnp.int32)
    order = jnp.where(slots < list_dev // 2, places[0], places[1]) * (list_dev // 8)
    relative_slots = jnp.where(slots < 0, -1, slots ^ order).reshape(STEPS, 1, owners * capacity)

    def sums_of(rows, step):
        return list_sums(rows, 0, relative_slots, step, list_dev)

    def residual(rows, step, parts, into=None, place=0, count=1):
        return residual_rows(
            rows, 0, slot_cols, step, centroids, weights, parts, places, into, place, count
        )

    second, third, slot_cols, weights, received0 = gate(second, third, slot_cols, weights, received0)
    received1 = exchange(second)

    done = scatter_sum(sums_of(received0, 0))
    buffer = residual(received0, 0, [], third, 1, 2)
    buffer, done, received1 = gate(buffer, done, received1)
    mixed = exchange(buffer)

    whole = gather_sum(done)
    parts = [whole]
    done = scatter_sum(sums_of(received1, 1))
    buffer = residual(received1, 1, parts)
    whole = gather_sum(done)
    buffer, whole, mixed = gate(buffer, whole, mixed)
    back1 = exchange(buffer)

    parts = parts + [whole]
    done = scatter_sum(sums_of(mixed, 2))
    buffer = residual(mixed, 2, parts)
    buffer, done, back1 = gate(buffer, done, back1)
    back2 = exchange(buffer)

    parts = parts + [gather_sum(done)]
    current = new_rows(centroids, weights, parts, places)
    output = unpack_rows(mixed, 1, dest_cols, 0, None, row_count)
    output = unpack_rows(back1, 0, dest_cols, 1, output, row_count)
    output = unpack_rows(back2, 0, dest_cols, 2, output, row_count)
    return (output, current)


def solution(mesh):
    in_specs = (
        P(None, ("grp", "list"), None),
        P(None, ("grp", "list"), None),
        P(None, ("grp", "list")),
        P("list", None),
        P("list"),
    )
    out_specs = (P(None, ("grp", "list"), None), P("list", None))
    return jax.shard_map(local, mesh=mesh, in_specs=in_specs, out_specs=out_specs, check_vma=False)
```

```python
import jax
import jax.numpy as jnp
from jax import lax
from jax.experimental import pallas as pl
from jax.experimental.pallas import tpu as pltpu
from jax.sharding import PartitionSpec as P

STEPS = 3
BLOCK = 512
CHEAP = pl.CostEstimate(flops=1, bytes_accessed=1, transcendentals=0)


def gate(*values):
    return lax.optimization_barrier(values)


def swap(rows, axis, offset):
    count = lax.axis_size(axis)
    return lax.ppermute(rows, axis, [(i, i ^ offset) for i in range(count)])


def select(hit):
    return jnp.where(hit, 1.0, 0.0).astype(jnp.bfloat16)


def mix(left, right):
    return jnp.dot(left, right, preferred_element_type=jnp.float32)


def pack_rows(vectors, dest, step, owners, capacity, count):
    row_count, width = vectors.shape[1:]
    group = BLOCK // capacity

    def body(dest_ref, vec_ref, out_ref):
        rows = lax.broadcasted_iota(jnp.int32, (BLOCK, row_count), 0) + pl.program_id(0) * BLOCK
        picked = mix(select(rows == dest_ref[0]), vec_ref[0]).astype(jnp.bfloat16)
        out_ref[...] = picked.reshape(group, 1, capacity, width)

    return pl.pallas_call(
        body,
        grid=(owners // group,),
        in_specs=[
            pl.BlockSpec((1, 1, row_count), lambda b: (step, 0, 0)),
            pl.BlockSpec((1, row_count, width), lambda b: (step, 0, 0)),
        ],
        out_specs=pl.BlockSpec((group, 1, capacity, width), lambda b: (b, 0, 0, 0)),
        out_shape=jax.ShapeDtypeStruct((owners, count, capacity, width), jnp.bfloat16),
        name="pack_rows",
        cost_estimate=CHEAP,
    )(dest, vectors)


def list_sums(received, at, slots, step, list_dev):
    owners, _, capacity, width = received.shape
    rows = owners * capacity
    sizes = [list_dev // 8, list_dev // 8, list_dev // 4] * 2

    def body(slot_ref, row_ref, *outs):
        data = row_ref[...].reshape(rows, width)
        first = 0
        for half in range(2):
            lists = lax.broadcasted_iota(jnp.int32, (list_dev // 2, rows), 0) + first
            sums = mix(select(lists == slot_ref[0]), data).astype(jnp.bfloat16)
            at = 0
            for out_ref in outs[3 * half : 3 * half + 3]:
                out_ref[...] = sums[at : at + out_ref.shape[0]]
                at += out_ref.shape[0]
            first += list_dev // 2

    return pl.pallas_call(
        body,
        grid=(1,),
        in_specs=[
            pl.BlockSpec((1, 1, rows), lambda i: (step, 0, 0)),
            pl.BlockSpec((owners, 1, capacity, width), lambda i: (0, at, 0, 0)),
        ],
        out_specs=[pl.BlockSpec((size, width), lambda i: (0, 0)) for size in sizes],
        out_shape=[jax.ShapeDtypeStruct((size, width), jnp.bfloat16) for size in sizes],
        name="list_sums",
        cost_estimate=CHEAP,
    )(slots, received)


def update(step, index, place_ref, weight_ref, table_ref, parts, store):
    chunk = table_ref.shape[0]
    slab = 16

    def run(piece, flip):
        def one(k, carry):
            at = pl.ds(pl.multiple_of(k * slab, slab), slab)
            table = table_ref[at, :]
            if parts:
                away = pl.ds(pl.multiple_of((k * slab) ^ flip, slab), slab)
                total = parts[0][piece][away, :].astype(jnp.float32)
                for four in parts[1:]:
                    total = total + four[piece][away, :].astype(jnp.float32)
                weights = weight_ref[at, :]
                share = 1.0 / weights[:, step : step + 1]
                table = (weights[:, :1] * table + total) * share
            store(index * chunk + k * slab, at, table)
            return carry

        lax.fori_loop(0, chunk // slab, one, 0, unroll=4)

    if not parts:
        run(0, 0)
        return
    half = index // 2
    place = place_ref[half]
    mine = 2 * half + ((index % 2) ^ (place // 2))
    for piece in range(4):
        pl.when(mine == piece)(lambda piece=piece: run(piece, (place % 2) * (chunk // 2)))


def part_specs(parts):
    return [pl.BlockSpec(p.shape, lambda i, group: (0, 0)) for four in parts for p in four]


def fours(refs):
    return [refs[k : k + 4] for k in range(0, len(refs), 4)]


def residual_rows(received, at, slots, step, centroids, weights, parts, places, into, place, count):
    owners, _, capacity, width = received.shape
    list_dev = centroids.shape[0]
    group = BLOCK // capacity
    blocks = owners // group
    chunks = 4
    chunk = list_dev // chunks
    part_count = 4 * len(parts)

    def body(place_ref, slot_ref, row_ref, table_ref, weight_ref, *rest):
        out_ref, pair_ref = rest[-2:]
        index = pl.program_id(0)

        def store(first, at, table):
            hi = table.astype(jnp.bfloat16)
            lo = (table - hi.astype(jnp.float32)).astype(jnp.bfloat16)
            pair_ref[pl.ds(pl.multiple_of(first, 16), 16), :] = hi
            pair_ref[pl.ds(pl.multiple_of(list_dev + first, 16), 16), :] = lo

        @pl.when(index < chunks)
        def _():
            update(step, index, place_ref, weight_ref, table_ref, fours(rest[:part_count]), store)

        @pl.when(index >= chunks)
        def _():
            lists = lax.broadcasted_iota(jnp.int32, (BLOCK, list_dev), 1)
            hit = select(lists == slot_ref[:, step : step + 1])
            chosen = mix(jnp.concatenate([hit, hit], axis=1), pair_ref[...])
            data = row_ref[...].reshape(BLOCK, width).astype(jnp.float32)
            out_ref[...] = (data - chosen).astype(jnp.bfloat16).reshape(group, 1, capacity, width)

    def late(i):
        return jnp.maximum(i - chunks, 0)

    def early(i):
        return jnp.minimum(i, chunks - 1)

    in_specs = [
        pl.BlockSpec((BLOCK, STEPS), lambda i, places: (late(i), 0)),
        pl.BlockSpec((group, 1, capacity, width), lambda i, places: (late(i), at, 0, 0)),
        pl.BlockSpec((chunk, width), lambda i, places: (early(i), 0)),
        pl.BlockSpec((chunk, STEPS + 1), lambda i, places: (early(i), 0)),
    ] + part_specs(parts)
    args = [slots, received, centroids, weights] + [p for four in parts for p in four]
    aliases = {}
    if into is not None:
        in_specs.append(pl.BlockSpec(memory_space=pl.ANY))
        aliases = {1 + len(args): 0}
        args.append(into)
    return pl.pallas_call(
        body,
        grid_spec=pltpu.PrefetchScalarGridSpec(
            num_scalar_prefetch=1,
            grid=(chunks + blocks,),
            in_specs=in_specs,
            out_specs=pl.BlockSpec(
                (group, 1, capacity, width), lambda i, places: (late(i), place, 0, 0)
            ),
            scratch_shapes=[pltpu.VMEM((2 * list_dev, width), jnp.bfloat16)],
        ),
        out_shape=jax.ShapeDtypeStruct((owners, count, capacity, width), jnp.bfloat16),
        input_output_aliases=aliases,
        name="residual_rows",
        cost_estimate=CHEAP,
    )(places, *args)


def new_rows(centroids, weights, parts, places, piece, into):
    list_dev, width = centroids.shape
    chunk = list_dev // 4
    slab = 16

    def body(place_ref, table_ref, weight_ref, *rest):
        half = pl.program_id(0)

        def run(which):
            flip = (place_ref[which] % 2) * (chunk // 2)

            def one(k, carry):
                at = pl.ds(pl.multiple_of(k * slab, slab), slab)
                away = pl.ds(pl.multiple_of((k * slab) ^ flip, slab), slab)
                total = rest[which][away, :].astype(jnp.float32)
                for four in range(1, STEPS):
                    total = total + rest[2 * four + which][away, :].astype(jnp.float32)
                block = weight_ref[at, :]
                share = 1.0 / block[:, STEPS : STEPS + 1]
                rest[-1][at, :] = (block[:, :1] * table_ref[at, :] + total) * share
                return carry

            lax.fori_loop(0, chunk // slab, one, 0, unroll=4)

        for which in range(2):
            pl.when(half == which)(lambda which=which: run(which))

    def chunk_of(i, places):
        return 2 * i + (piece ^ (places[i] // 2))

    pieces = [four[2 * half + piece] for four in parts for half in range(2)]
    in_specs = [
        pl.BlockSpec((chunk, width), lambda i, places: (chunk_of(i, places), 0)),
        pl.BlockSpec((chunk, STEPS + 1), lambda i, places: (chunk_of(i, places), 0)),
    ] + [pl.BlockSpec(p.shape, lambda i, places: (0, 0)) for p in pieces]
    args = [centroids, weights] + pieces
    aliases = {}
    if into is not None:
        in_specs.append(pl.BlockSpec(memory_space=pl.ANY))
        aliases = {1 + len(args): 0}
        args.append(into)
    return pl.pallas_call(
        body,
        grid_spec=pltpu.PrefetchScalarGridSpec(
            num_scalar_prefetch=1,
            grid=(2,),
            in_specs=in_specs,
            out_specs=pl.BlockSpec((chunk, width), lambda i, places: (chunk_of(i, places), 0)),
        ),
        out_shape=jax.ShapeDtypeStruct((list_dev, width), jnp.float32),
        input_output_aliases=aliases,
        name="new_rows",
        cost_estimate=CHEAP,
    )(places, *args)


def unpack_rows(back, at, dest, step, into, row_count):
    owners, _, capacity, width = back.shape
    rows = owners * capacity

    def body(dest_ref, row_ref, *rest):
        places = lax.broadcasted_iota(jnp.int32, (row_count, rows), 1)
        data = row_ref[...].reshape(rows, width)
        hit = select(places == dest_ref[:, step : step + 1])
        rest[-1][0] = mix(hit, data).astype(jnp.bfloat16)

    in_specs = [
        pl.BlockSpec((row_count, STEPS), lambda b: (0, 0)),
        pl.BlockSpec((owners, 1, capacity, width), lambda b: (0, at, 0, 0)),
    ]
    args = [dest, back]
    aliases = {}
    if into is not None:
        in_specs.append(pl.BlockSpec(memory_space=pl.ANY))
        args.append(into)
        aliases = {2: 0}
    return pl.pallas_call(
        body,
        grid=(1,),
        in_specs=in_specs,
        out_specs=pl.BlockSpec((1, row_count, width), lambda b: (step, 0, 0)),
        out_shape=jax.ShapeDtypeStruct((STEPS, row_count, width), jnp.bfloat16),
        input_output_aliases=aliases,
        name="unpack_rows",
        cost_estimate=CHEAP,
    )(*args)


def add(*values):
    total = values[0].astype(jnp.float32)
    for value in values[1:]:
        total = total + value.astype(jnp.float32)
    return total.astype(jnp.bfloat16)


def send_far(parts):
    return [swap(parts[2], "grp", 1), swap(parts[5], "grp", 3)]


def send_near(parts, got):
    block = parts[0].shape[0]
    over = [swap(add(parts[3 * h + 1], got[h][block:]), "grp", 3 - 2 * h) for h in range(2)]
    return [add(parts[3 * h], got[h][:block], over[h]) for h in range(2)]


def spread_near(done):
    return [jnp.concatenate([done[h], swap(done[h], "grp", 3 - 2 * h)]) for h in range(2)]


def spread_far(own):
    near = [swap(own[h], "grp", 1 + 2 * h) for h in range(2)]
    return [own[0], near[0], own[1], near[1]]


def exchange(rows):
    return lax.all_to_all(rows, "list", split_axis=0, concat_axis=0, tiled=True)


def local(vectors, owner_route, list_slot, centroids, counts):
    owners = lax.axis_size("list")
    grp_count = lax.axis_size("grp")
    row_count = vectors.shape[1]
    capacity = 2 * row_count // owners
    list_dev = centroids.shape[0]
    group = lax.axis_index("grp")
    assert grp_count == 4

    owner_ids = owner_route[:, :, 0]
    hits = owner_ids[:, None, :] == jnp.arange(owners, dtype=jnp.int32)[None, :, None]
    earlier = jnp.arange(row_count)[:, None] < jnp.arange(row_count)[None, :]
    rank = mix(
        hits.reshape(STEPS * owners, row_count).astype(jnp.bfloat16), earlier.astype(jnp.bfloat16)
    )
    rank = jnp.sum(jnp.where(hits, rank.reshape(hits.shape), 0.0), axis=1).astype(jnp.int32)
    dest = owner_ids * capacity + rank
    dest_lanes = dest.reshape(STEPS, 1, row_count)

    places = jnp.arange(owners * capacity, dtype=jnp.int32)
    found = dest[:, None, :] == places[None, :, None]
    slots = jnp.sum(jnp.where(found, list_slot[:, None, :] + 1, 0), axis=2) - 1
    slots = slots.reshape(STEPS, owners, capacity).transpose(1, 0, 2)
    slots = exchange(slots.reshape(owners, 1, STEPS * capacity))

    first = pack_rows(vectors, dest_lanes, 0, owners, capacity, 1)
    first, slots = gate(first, slots)
    received0 = exchange(first)
    second = pack_rows(vectors, dest_lanes, 1, owners, capacity, 1)
    third = pack_rows(vectors, dest_lanes, 2, owners, capacity, 2)

    slots = slots.reshape(owners, STEPS, capacity).transpose(1, 0, 2)
    slots = slots.reshape(STEPS, owners * capacity)
    slot_cols = slots.T
    dest_cols = dest.T

    list_iota = jnp.arange(list_dev, dtype=jnp.int32)
    batch = jnp.sum((slots[:, None, :] == list_iota[None, :, None]).astype(jnp.int32), axis=2)
    batch = sum([batch] + [swap(batch, "grp", offset) for offset in range(1, grp_count)])
    weights = [counts]
    for step in range(STEPS):
        weights.append(weights[-1] + batch[step])
    weights = jnp.stack(weights).astype(jnp.float32).T

    high = group // 2
    low = (group ^ high) % 2
    places = jnp.stack([2 * low + high, 2 * high + low]).astype(jnp.int32)
    order = jnp.where(slots < list_dev // 2, places[0], places[1]) * (list_dev // 8)
    relative_slots = jnp.where(slots < 0, -1, slots ^ order).reshape(STEPS, 1, owners * capacity)

    def sums_of(rows, step):
        return list_sums(rows, 0, relative_slots, step, list_dev)

    def residual(rows, step, parts, into=None, place=0, count=1):
        return residual_rows(
            rows, 0, slot_cols, step, centroids, weights, parts, places, into, place, count
        )

    second, third, slot_cols, weights, received0 = gate(second, third, slot_cols, weights, received0)
    received1 = exchange(second)

    sums = sums_of(received0, 0)
    got = send_far(sums)
    buffer = residual(received0, 0, [], third, 1, 2)
    buffer, got = gate(buffer, got)
    done = send_near(sums, got)
    buffer, done, received1 = gate(buffer, done, received1)
    mixed = exchange(buffer)

    own = spread_near(done)
    received1, own = gate(received1, own)
    whole = spread_far(own)
    sums = sums_of(received1, 1)
    sums, whole = gate(sums, whole)
    parts = [whole]
    got = send_far(sums)
    buffer = residual(received1, 1, parts)
    buffer, got = gate(buffer, got)
    own = spread_near(send_near(sums, got))
    buffer, own, mixed = gate(buffer, own, mixed)
    back1 = exchange(buffer)

    parts = parts + [spread_far(own)]
    sums = sums_of(mixed, 2)
    got = send_far(sums)
    buffer = residual(mixed, 2, parts)
    buffer, got, back1 = gate(buffer, got, back1)
    back2 = exchange(buffer)

    parts = parts + [spread_far(spread_near(send_near(sums, got)))]
    current = new_rows(centroids, weights, parts, places, 0, None)
    current = new_rows(centroids, weights, parts, places, 1, current)
    output = unpack_rows(mixed, 1, dest_cols, 0, None, row_count)
    output = unpack_rows(back1, 0, dest_cols, 1, output, row_count)
    output = unpack_rows(back2, 0, dest_cols, 2, output, row_count)
    return (output, current)


def solution(mesh):
    in_specs = (
        P(None, ("grp", "list"), None),
        P(None, ("grp", "list"), None),
        P(None, ("grp", "list")),
        P("list", None),
        P("list"),
    )
    out_specs = (P(None, ("grp", "list"), None), P("list", None))
    return jax.shard_map(local, mesh=mesh, in_specs=in_specs, out_specs=out_specs, check_vma=False)
```

```python
import jax
import jax.numpy as jnp
from jax import lax
from jax.experimental import pallas as pl
from jax.experimental.pallas import tpu as pltpu
from jax.sharding import PartitionSpec as P

STEPS = 3
BLOCK = 512
CHEAP = pl.CostEstimate(flops=1, bytes_accessed=1, transcendentals=0)


def gate(*values):
    return lax.optimization_barrier(values)


def swap(rows, axis, offset):
    count = lax.axis_size(axis)
    return lax.ppermute(rows, axis, [(i, i ^ offset) for i in range(count)])


def select(hit):
    return jnp.where(hit, 1.0, 0.0).astype(jnp.bfloat16)


def mix(left, right):
    return jnp.dot(left, right, preferred_element_type=jnp.float32)


def pack_rows(vectors, dest, step, owners, capacity, count):
    row_count, width = vectors.shape[1:]
    group = BLOCK // capacity

    def body(dest_ref, vec_ref, out_ref):
        rows = lax.broadcasted_iota(jnp.int32, (BLOCK, row_count), 0) + pl.program_id(0) * BLOCK
        picked = mix(select(rows == dest_ref[0]), vec_ref[0]).astype(jnp.bfloat16)
        out_ref[...] = picked.reshape(group, 1, capacity, width)

    return pl.pallas_call(
        body,
        grid=(owners // group,),
        in_specs=[
            pl.BlockSpec((1, 1, row_count), lambda b: (step, 0, 0)),
            pl.BlockSpec((1, row_count, width), lambda b: (step, 0, 0)),
        ],
        out_specs=pl.BlockSpec((group, 1, capacity, width), lambda b: (b, 0, 0, 0)),
        out_shape=jax.ShapeDtypeStruct((owners, count, capacity, width), jnp.bfloat16),
        name="pack_rows",
        cost_estimate=CHEAP,
    )(dest, vectors)


def list_sums(received, at, slots, step, list_dev):
    owners, _, capacity, width = received.shape
    rows = owners * capacity
    sizes = [list_dev // 8, list_dev // 8, list_dev // 4] * 2

    def body(slot_ref, row_ref, *outs):
        data = row_ref[...].reshape(rows, width)
        first = 0
        for half in range(2):
            lists = lax.broadcasted_iota(jnp.int32, (list_dev // 2, rows), 0) + first
            sums = mix(select(lists == slot_ref[0]), data).astype(jnp.bfloat16)
            at = 0
            for out_ref in outs[3 * half : 3 * half + 3]:
                out_ref[...] = sums[at : at + out_ref.shape[0]]
                at += out_ref.shape[0]
            first += list_dev // 2

    return pl.pallas_call(
        body,
        grid=(1,),
        in_specs=[
            pl.BlockSpec((1, 1, rows), lambda i: (step, 0, 0)),
            pl.BlockSpec((owners, 1, capacity, width), lambda i: (0, at, 0, 0)),
        ],
        out_specs=[pl.BlockSpec((size, width), lambda i: (0, 0)) for size in sizes],
        out_shape=[jax.ShapeDtypeStruct((size, width), jnp.bfloat16) for size in sizes],
        name="list_sums",
        cost_estimate=CHEAP,
    )(slots, received)


def update(step, index, place_ref, weight_ref, table_ref, parts, store):
    chunk = table_ref.shape[0]
    slab = 16

    def run(piece, flip):
        def one(k, carry):
            at = pl.ds(pl.multiple_of(k * slab, slab), slab)
            table = table_ref[at, :]
            if parts:
                away = pl.ds(pl.multiple_of((k * slab) ^ flip, slab), slab)
                total = parts[0][piece][away, :].astype(jnp.float32)
                for four in parts[1:]:
                    total = total + four[piece][away, :].astype(jnp.float32)
                weights = weight_ref[at, :]
                share = 1.0 / weights[:, step : step + 1]
                table = (weights[:, :1] * table + total) * share
            store(index * chunk + k * slab, at, table)
            return carry

        lax.fori_loop(0, chunk // slab, one, 0, unroll=4)

    if not parts:
        run(0, 0)
        return
    half = index // 2
    place = place_ref[half]
    mine = 2 * half + ((index % 2) ^ (place // 2))
    for piece in range(4):
        pl.when(mine == piece)(lambda piece=piece: run(piece, (place % 2) * (chunk // 2)))


def part_specs(parts):
    return [pl.BlockSpec(p.shape, lambda i, group: (0, 0)) for four in parts for p in four]


def fours(refs):
    return [refs[k : k + 4] for k in range(0, len(refs), 4)]


def residual_rows(received, at, slots, step, centroids, weights, parts, places, into, place, count):
    owners, _, capacity, width = received.shape
    list_dev = centroids.shape[0]
    group = BLOCK // capacity
    blocks = owners // group
    chunks = 4
    chunk = list_dev // chunks
    part_count = 4 * len(parts)

    def body(place_ref, slot_ref, row_ref, table_ref, weight_ref, *rest):
        out_ref, pair_ref = rest[-2:]
        index = pl.program_id(0)

        def store(first, at, table):
            hi = table.astype(jnp.bfloat16)
            lo = (table - hi.astype(jnp.float32)).astype(jnp.bfloat16)
            pair_ref[pl.ds(pl.multiple_of(first, 16), 16), :] = hi
            pair_ref[pl.ds(pl.multiple_of(list_dev + first, 16), 16), :] = lo

        @pl.when(index < chunks)
        def _():
            update(step, index, place_ref, weight_ref, table_ref, fours(rest[:part_count]), store)

        @pl.when(index >= chunks)
        def _():
            lists = lax.broadcasted_iota(jnp.int32, (BLOCK, list_dev), 1)
            hit = select(lists == slot_ref[:, step : step + 1])
            chosen = mix(jnp.concatenate([hit, hit], axis=1), pair_ref[...])
            data = row_ref[...].reshape(BLOCK, width).astype(jnp.float32)
            out_ref[...] = (data - chosen).astype(jnp.bfloat16).reshape(group, 1, capacity, width)

    def late(i):
        return jnp.maximum(i - chunks, 0)

    def early(i):
        return jnp.minimum(i, chunks - 1)

    in_specs = [
        pl.BlockSpec((BLOCK, STEPS), lambda i, places: (late(i), 0)),
        pl.BlockSpec((group, 1, capacity, width), lambda i, places: (late(i), at, 0, 0)),
        pl.BlockSpec((chunk, width), lambda i, places: (early(i), 0)),
        pl.BlockSpec((chunk, STEPS + 1), lambda i, places: (early(i), 0)),
    ] + part_specs(parts)
    args = [slots, received, centroids, weights] + [p for four in parts for p in four]
    aliases = {}
    if into is not None:
        in_specs.append(pl.BlockSpec(memory_space=pl.ANY))
        aliases = {1 + len(args): 0}
        args.append(into)
    return pl.pallas_call(
        body,
        grid_spec=pltpu.PrefetchScalarGridSpec(
            num_scalar_prefetch=1,
            grid=(chunks + blocks,),
            in_specs=in_specs,
            out_specs=pl.BlockSpec(
                (group, 1, capacity, width), lambda i, places: (late(i), place, 0, 0)
            ),
            scratch_shapes=[pltpu.VMEM((2 * list_dev, width), jnp.bfloat16)],
        ),
        out_shape=jax.ShapeDtypeStruct((owners, count, capacity, width), jnp.bfloat16),
        input_output_aliases=aliases,
        name="residual_rows",
        cost_estimate=CHEAP,
    )(places, *args)


def new_rows(centroids, weights, parts, places, piece, into):
    list_dev, width = centroids.shape
    chunk = list_dev // 4
    slab = 16

    def body(place_ref, table_ref, weight_ref, *rest):
        half = pl.program_id(0)

        def run(which):
            flip = (place_ref[which] % 2) * (chunk // 2)

            def one(k, carry):
                at = pl.ds(pl.multiple_of(k * slab, slab), slab)
                away = pl.ds(pl.multiple_of((k * slab) ^ flip, slab), slab)
                total = rest[which][away, :].astype(jnp.float32)
                for four in range(1, STEPS):
                    total = total + rest[2 * four + which][away, :].astype(jnp.float32)
                block = weight_ref[at, :]
                share = 1.0 / block[:, STEPS : STEPS + 1]
                rest[-1][at, :] = (block[:, :1] * table_ref[at, :] + total) * share
                return carry

            lax.fori_loop(0, chunk // slab, one, 0, unroll=4)

        for which in range(2):
            pl.when(half == which)(lambda which=which: run(which))

    def chunk_of(i, places):
        return 2 * i + (piece ^ (places[i] // 2))

    pieces = [four[2 * half + piece] for four in parts for half in range(2)]
    in_specs = [
        pl.BlockSpec((chunk, width), lambda i, places: (chunk_of(i, places), 0)),
        pl.BlockSpec((chunk, STEPS + 1), lambda i, places: (chunk_of(i, places), 0)),
    ] + [pl.BlockSpec(p.shape, lambda i, places: (0, 0)) for p in pieces]
    args = [centroids, weights] + pieces
    aliases = {}
    if into is not None:
        in_specs.append(pl.BlockSpec(memory_space=pl.ANY))
        aliases = {1 + len(args): 0}
        args.append(into)
    return pl.pallas_call(
        body,
        grid_spec=pltpu.PrefetchScalarGridSpec(
            num_scalar_prefetch=1,
            grid=(2,),
            in_specs=in_specs,
            out_specs=pl.BlockSpec((chunk, width), lambda i, places: (chunk_of(i, places), 0)),
        ),
        out_shape=jax.ShapeDtypeStruct((list_dev, width), jnp.float32),
        input_output_aliases=aliases,
        name="new_rows",
        cost_estimate=CHEAP,
    )(places, *args)


def unpack_rows(back, at, dest, step, into, row_count):
    owners, _, capacity, width = back.shape
    rows = owners * capacity

    def body(dest_ref, row_ref, *rest):
        places = lax.broadcasted_iota(jnp.int32, (row_count, rows), 1)
        data = row_ref[...].reshape(rows, width)
        hit = select(places == dest_ref[:, step : step + 1])
        rest[-1][0] = mix(hit, data).astype(jnp.bfloat16)

    in_specs = [
        pl.BlockSpec((row_count, STEPS), lambda b: (0, 0)),
        pl.BlockSpec((owners, 1, capacity, width), lambda b: (0, at, 0, 0)),
    ]
    args = [dest, back]
    aliases = {}
    if into is not None:
        in_specs.append(pl.BlockSpec(memory_space=pl.ANY))
        args.append(into)
        aliases = {2: 0}
    return pl.pallas_call(
        body,
        grid=(1,),
        in_specs=in_specs,
        out_specs=pl.BlockSpec((1, row_count, width), lambda b: (step, 0, 0)),
        out_shape=jax.ShapeDtypeStruct((STEPS, row_count, width), jnp.bfloat16),
        input_output_aliases=aliases,
        name="unpack_rows",
        cost_estimate=CHEAP,
    )(*args)


def add(*values):
    total = values[0].astype(jnp.float32)
    for value in values[1:]:
        total = total + value.astype(jnp.float32)
    return total.astype(jnp.bfloat16)


def send_far(parts):
    return [swap(parts[2], "grp", 1), swap(parts[5], "grp", 3)]


def send_near(parts, got):
    block = parts[0].shape[0]
    over = [swap(add(parts[3 * h + 1], got[h][block:]), "grp", 3 - 2 * h) for h in range(2)]
    return [add(parts[3 * h], got[h][:block], over[h]) for h in range(2)]


def spread_near(done):
    return [jnp.concatenate([done[h], swap(done[h], "grp", 3 - 2 * h)]) for h in range(2)]


def spread_far(own):
    near = [swap(own[h], "grp", 1 + 2 * h) for h in range(2)]
    return [own[0], near[0], own[1], near[1]]


def exchange(rows):
    return lax.all_to_all(rows, "list", split_axis=0, concat_axis=0, tiled=True)


def local(vectors, owner_route, list_slot, centroids, counts):
    owners = lax.axis_size("list")
    grp_count = lax.axis_size("grp")
    row_count = vectors.shape[1]
    capacity = 2 * row_count // owners
    list_dev = centroids.shape[0]
    group = lax.axis_index("grp")
    assert grp_count == 4

    owner_ids = owner_route[:, :, 0]
    hits = owner_ids[:, None, :] == jnp.arange(owners, dtype=jnp.int32)[None, :, None]
    earlier = jnp.arange(row_count)[:, None] < jnp.arange(row_count)[None, :]
    rank = mix(
        hits.reshape(STEPS * owners, row_count).astype(jnp.bfloat16), earlier.astype(jnp.bfloat16)
    )
    rank = jnp.sum(jnp.where(hits, rank.reshape(hits.shape), 0.0), axis=1).astype(jnp.int32)
    dest = owner_ids * capacity + rank
    dest_lanes = dest.reshape(STEPS, 1, row_count)

    places = jnp.arange(owners * capacity, dtype=jnp.int32)
    found = dest[:, None, :] == places[None, :, None]
    slots = jnp.sum(jnp.where(found, list_slot[:, None, :] + 1, 0), axis=2) - 1
    slots = slots.reshape(STEPS, owners, capacity).transpose(1, 0, 2)
    slots = exchange(slots.reshape(owners, 1, STEPS * capacity))

    first = pack_rows(vectors, dest_lanes, 0, owners, capacity, 1)
    first, slots = gate(first, slots)
    received0 = exchange(first)
    second = pack_rows(vectors, dest_lanes, 1, owners, capacity, 1)
    third = pack_rows(vectors, dest_lanes, 2, owners, capacity, 2)

    slots = slots.reshape(owners, STEPS, capacity).transpose(1, 0, 2)
    slots = slots.reshape(STEPS, owners * capacity)
    slot_cols = slots.T
    dest_cols = dest.T

    list_iota = jnp.arange(list_dev, dtype=jnp.int32)
    batch = jnp.sum((slots[:, None, :] == list_iota[None, :, None]).astype(jnp.int32), axis=2)
    batch = sum([batch] + [swap(batch, "grp", offset) for offset in range(1, grp_count)])
    weights = [counts]
    for step in range(STEPS):
        weights.append(weights[-1] + batch[step])
    weights = jnp.stack(weights).astype(jnp.float32).T

    high = group // 2
    low = (group ^ high) % 2
    places = jnp.stack([2 * low + high, 2 * high + low]).astype(jnp.int32)
    order = jnp.where(slots < list_dev // 2, places[0], places[1]) * (list_dev // 8)
    relative_slots = jnp.where(slots < 0, -1, slots ^ order).reshape(STEPS, 1, owners * capacity)

    def sums_of(rows, step):
        return list_sums(rows, 0, relative_slots, step, list_dev)

    def residual(rows, step, parts, into=None, place=0, count=1):
        return residual_rows(
            rows, 0, slot_cols, step, centroids, weights, parts, places, into, place, count
        )

    second, third, slot_cols, weights, received0 = gate(second, third, slot_cols, weights, received0)
    received1 = exchange(second)

    sums = sums_of(received0, 0)
    got = send_far(sums)
    buffer = residual(received0, 0, [], third, 1, 2)
    buffer, got = gate(buffer, got)
    done = send_near(sums, got)
    buffer, done, received1 = gate(buffer, done, received1)
    mixed = exchange(buffer)

    own = spread_near(done)
    received1, own = gate(received1, own)
    whole = spread_far(own)
    sums = sums_of(received1, 1)
    sums, whole = gate(sums, whole)
    parts = [whole]
    got = send_far(sums)
    buffer = residual(received1, 1, parts)
    buffer, got = gate(buffer, got)
    own = spread_near(send_near(sums, got))
    buffer, own, mixed = gate(buffer, own, mixed)
    back1 = exchange(buffer)

    parts = parts + [spread_far(own)]
    sums = sums_of(mixed, 2)
    got = send_far(sums)
    buffer = residual(mixed, 2, parts)
    output = unpack_rows(mixed, 1, dest_cols, 0, None, row_count)
    buffer, got, output, back1 = gate(buffer, got, output, back1)
    back2 = exchange(buffer)

    whole = spread_far(spread_near(send_near(sums, got)))
    current = new_rows(centroids, weights, parts + [whole], places, 0, None)
    output = unpack_rows(back1, 0, dest_cols, 1, output, row_count)
    output, current = gate(output, current)
    output = unpack_rows(back2, 0, dest_cols, 2, output, row_count)
    output, whole[1], whole[3] = gate(output, whole[1], whole[3])
    current = new_rows(centroids, weights, parts + [whole], places, 1, current)
    return (output, current)


def solution(mesh):
    in_specs = (
        P(None, ("grp", "list"), None),
        P(None, ("grp", "list"), None),
        P(None, ("grp", "list")),
        P("list", None),
        P("list"),
    )
    out_specs = (P(None, ("grp", "list"), None), P("list", None))
    return jax.shard_map(local, mesh=mesh, in_specs=in_specs, out_specs=out_specs, check_vma=False)
```

```python
import jax
import jax.numpy as jnp
from jax import lax
from jax.experimental import pallas as pl
from jax.experimental.pallas import tpu as pltpu
from jax.sharding import PartitionSpec as P

STEPS = 3
BLOCK = 512
CHEAP = pl.CostEstimate(flops=1, bytes_accessed=1, transcendentals=0)


def gate(*values):
    return lax.optimization_barrier(values)


def swap(rows, axis, offset):
    count = lax.axis_size(axis)
    return lax.ppermute(rows, axis, [(i, i ^ offset) for i in range(count)])


def select(hit):
    return jnp.where(hit, 1.0, 0.0).astype(jnp.bfloat16)


def mix(left, right):
    return jnp.dot(left, right, preferred_element_type=jnp.float32)


def pack_rows(vectors, dest, step, owners, capacity, count):
    row_count, width = vectors.shape[1:]
    group = BLOCK // capacity

    def body(dest_ref, vec_ref, out_ref):
        rows = lax.broadcasted_iota(jnp.int32, (BLOCK, row_count), 0) + pl.program_id(0) * BLOCK
        picked = mix(select(rows == dest_ref[0]), vec_ref[0]).astype(jnp.bfloat16)
        out_ref[...] = picked.reshape(group, 1, capacity, width)

    return pl.pallas_call(
        body,
        grid=(owners // group,),
        in_specs=[
            pl.BlockSpec((1, 1, row_count), lambda b: (step, 0, 0)),
            pl.BlockSpec((1, row_count, width), lambda b: (step, 0, 0)),
        ],
        out_specs=pl.BlockSpec((group, 1, capacity, width), lambda b: (b, 0, 0, 0)),
        out_shape=jax.ShapeDtypeStruct((owners, count, capacity, width), jnp.bfloat16),
        name="pack_rows",
        cost_estimate=CHEAP,
    )(dest, vectors)


def list_sums(received, at, slots, step, list_dev):
    owners, _, capacity, width = received.shape
    rows = owners * capacity
    sizes = [list_dev // 8, list_dev // 8, list_dev // 4] * 2

    def body(slot_ref, row_ref, *outs):
        data = row_ref[...].reshape(rows, width)
        first = 0
        for half in range(2):
            lists = lax.broadcasted_iota(jnp.int32, (list_dev // 2, rows), 0) + first
            sums = mix(select(lists == slot_ref[0]), data).astype(jnp.bfloat16)
            at = 0
            for out_ref in outs[3 * half : 3 * half + 3]:
                out_ref[...] = sums[at : at + out_ref.shape[0]]
                at += out_ref.shape[0]
            first += list_dev // 2

    return pl.pallas_call(
        body,
        grid=(1,),
        in_specs=[
            pl.BlockSpec((1, 1, rows), lambda i: (step, 0, 0)),
            pl.BlockSpec((owners, 1, capacity, width), lambda i: (0, at, 0, 0)),
        ],
        out_specs=[pl.BlockSpec(memory_space=pltpu.VMEM) for _ in sizes],
        out_shape=[pltpu.VMEM((size, width), jnp.bfloat16) for size in sizes],
        name="list_sums",
        cost_estimate=CHEAP,
    )(slots, received)


def update(step, index, place_ref, weight_ref, table_ref, parts, store):
    chunk = table_ref.shape[0]
    slab = 16

    def run(piece, flip):
        def one(k, carry):
            at = pl.ds(pl.multiple_of(k * slab, slab), slab)
            table = table_ref[at, :]
            if parts:
                away = pl.ds(pl.multiple_of((k * slab) ^ flip, slab), slab)
                total = parts[0][piece][away, :].astype(jnp.float32)
                for four in parts[1:]:
                    total = total + four[piece][away, :].astype(jnp.float32)
                weights = weight_ref[at, :]
                share = 1.0 / weights[:, step : step + 1]
                table = (weights[:, :1] * table + total) * share
            store(index * chunk + k * slab, at, table)
            return carry

        lax.fori_loop(0, chunk // slab, one, 0, unroll=4)

    if not parts:
        run(0, 0)
        return
    half = index // 2
    place = place_ref[half]
    mine = 2 * half + ((index % 2) ^ (place // 2))
    for piece in range(4):
        pl.when(mine == piece)(lambda piece=piece: run(piece, (place % 2) * (chunk // 2)))


def part_specs(parts):
    return [pl.BlockSpec(p.shape, lambda i, group: (0, 0)) for four in parts for p in four]


def fours(refs):
    return [refs[k : k + 4] for k in range(0, len(refs), 4)]


def residual_rows(received, at, slots, step, centroids, weights, parts, places, into, place, count):
    owners, _, capacity, width = received.shape
    list_dev = centroids.shape[0]
    group = BLOCK // capacity
    blocks = owners // group
    chunks = 4
    chunk = list_dev // chunks
    part_count = 4 * len(parts)

    def body(place_ref, slot_ref, row_ref, table_ref, weight_ref, *rest):
        out_ref, pair_ref = rest[-2:]
        index = pl.program_id(0)

        def store(first, at, table):
            hi = table.astype(jnp.bfloat16)
            lo = (table - hi.astype(jnp.float32)).astype(jnp.bfloat16)
            pair_ref[pl.ds(pl.multiple_of(first, 16), 16), :] = hi
            pair_ref[pl.ds(pl.multiple_of(list_dev + first, 16), 16), :] = lo

        @pl.when(index < chunks)
        def _():
            update(step, index, place_ref, weight_ref, table_ref, fours(rest[:part_count]), store)

        @pl.when(index >= chunks)
        def _():
            lists = lax.broadcasted_iota(jnp.int32, (BLOCK, list_dev), 1)
            hit = select(lists == slot_ref[:, step : step + 1])
            chosen = mix(jnp.concatenate([hit, hit], axis=1), pair_ref[...])
            data = row_ref[...].reshape(BLOCK, width).astype(jnp.float32)
            out_ref[...] = (data - chosen).astype(jnp.bfloat16).reshape(group, 1, capacity, width)

    def late(i):
        return jnp.maximum(i - chunks, 0)

    def early(i):
        return jnp.minimum(i, chunks - 1)

    in_specs = [
        pl.BlockSpec((BLOCK, STEPS), lambda i, places: (late(i), 0)),
        pl.BlockSpec((group, 1, capacity, width), lambda i, places: (late(i), at, 0, 0)),
        pl.BlockSpec((chunk, width), lambda i, places: (early(i), 0)),
        pl.BlockSpec((chunk, STEPS + 1), lambda i, places: (early(i), 0)),
    ] + part_specs(parts)
    args = [slots, received, centroids, weights] + [p for four in parts for p in four]
    aliases = {}
    if into is not None:
        in_specs.append(pl.BlockSpec(memory_space=pl.ANY))
        aliases = {1 + len(args): 0}
        args.append(into)
    return pl.pallas_call(
        body,
        grid_spec=pltpu.PrefetchScalarGridSpec(
            num_scalar_prefetch=1,
            grid=(chunks + blocks,),
            in_specs=in_specs,
            out_specs=pl.BlockSpec(
                (group, 1, capacity, width), lambda i, places: (late(i), place, 0, 0)
            ),
            scratch_shapes=[pltpu.VMEM((2 * list_dev, width), jnp.bfloat16)],
        ),
        out_shape=jax.ShapeDtypeStruct((owners, count, capacity, width), jnp.bfloat16),
        input_output_aliases=aliases,
        name="residual_rows",
        cost_estimate=CHEAP,
    )(places, *args)


def new_rows(centroids, weights, parts, places, piece, into):
    list_dev, width = centroids.shape
    chunk = list_dev // 4
    slab = 16

    def body(place_ref, table_ref, weight_ref, *rest):
        half = pl.program_id(0)

        def run(which):
            flip = (place_ref[which] % 2) * (chunk // 2)

            def one(k, carry):
                at = pl.ds(pl.multiple_of(k * slab, slab), slab)
                away = pl.ds(pl.multiple_of((k * slab) ^ flip, slab), slab)
                total = rest[which][away, :].astype(jnp.float32)
                for four in range(1, STEPS):
                    total = total + rest[2 * four + which][away, :].astype(jnp.float32)
                block = weight_ref[at, :]
                share = 1.0 / block[:, STEPS : STEPS + 1]
                rest[-1][at, :] = (block[:, :1] * table_ref[at, :] + total) * share
                return carry

            lax.fori_loop(0, chunk // slab, one, 0, unroll=4)

        for which in range(2):
            pl.when(half == which)(lambda which=which: run(which))

    def chunk_of(i, places):
        return 2 * i + (piece ^ (places[i] // 2))

    pieces = [four[2 * half + piece] for four in parts for half in range(2)]
    in_specs = [
        pl.BlockSpec((chunk, width), lambda i, places: (chunk_of(i, places), 0)),
        pl.BlockSpec((chunk, STEPS + 1), lambda i, places: (chunk_of(i, places), 0)),
    ] + [pl.BlockSpec(p.shape, lambda i, places: (0, 0)) for p in pieces]
    args = [centroids, weights] + pieces
    aliases = {}
    if into is not None:
        in_specs.append(pl.BlockSpec(memory_space=pl.ANY))
        aliases = {1 + len(args): 0}
        args.append(into)
    return pl.pallas_call(
        body,
        grid_spec=pltpu.PrefetchScalarGridSpec(
            num_scalar_prefetch=1,
            grid=(2,),
            in_specs=in_specs,
            out_specs=pl.BlockSpec((chunk, width), lambda i, places: (chunk_of(i, places), 0)),
        ),
        out_shape=jax.ShapeDtypeStruct((list_dev, width), jnp.float32),
        input_output_aliases=aliases,
        name="new_rows",
        cost_estimate=CHEAP,
    )(places, *args)


def unpack_rows(back, at, dest, step, into, row_count):
    owners, _, capacity, width = back.shape
    rows = owners * capacity

    def body(dest_ref, row_ref, *rest):
        places = lax.broadcasted_iota(jnp.int32, (row_count, rows), 1)
        data = row_ref[...].reshape(rows, width)
        hit = select(places == dest_ref[:, step : step + 1])
        rest[-1][0] = mix(hit, data).astype(jnp.bfloat16)

    in_specs = [
        pl.BlockSpec((row_count, STEPS), lambda b: (0, 0)),
        pl.BlockSpec((owners, 1, capacity, width), lambda b: (0, at, 0, 0)),
    ]
    args = [dest, back]
    aliases = {}
    if into is not None:
        in_specs.append(pl.BlockSpec(memory_space=pl.ANY))
        args.append(into)
        aliases = {2: 0}
    return pl.pallas_call(
        body,
        grid=(1,),
        in_specs=in_specs,
        out_specs=pl.BlockSpec((1, row_count, width), lambda b: (step, 0, 0)),
        out_shape=jax.ShapeDtypeStruct((STEPS, row_count, width), jnp.bfloat16),
        input_output_aliases=aliases,
        name="unpack_rows",
        cost_estimate=CHEAP,
    )(*args)


def add(*values):
    total = values[0].astype(jnp.float32)
    for value in values[1:]:
        total = total + value.astype(jnp.float32)
    return total.astype(jnp.bfloat16)


def send_far(parts):
    return [swap(parts[2], "grp", 1), swap(parts[5], "grp", 3)]


def send_near(parts, got):
    block = parts[0].shape[0]
    over = [swap(add(parts[3 * h + 1], got[h][block:]), "grp", 3 - 2 * h) for h in range(2)]
    return [add(parts[3 * h], got[h][:block], over[h]) for h in range(2)]


def spread_near(done):
    return [jnp.concatenate([done[h], swap(done[h], "grp", 3 - 2 * h)]) for h in range(2)]


def spread_far(own):
    near = [swap(own[h], "grp", 1 + 2 * h) for h in range(2)]
    return [own[0], near[0], own[1], near[1]]


def exchange(rows):
    return lax.all_to_all(rows, "list", split_axis=0, concat_axis=0, tiled=True)


def local(vectors, owner_route, list_slot, centroids, counts):
    owners = lax.axis_size("list")
    grp_count = lax.axis_size("grp")
    row_count = vectors.shape[1]
    capacity = 2 * row_count // owners
    list_dev = centroids.shape[0]
    group = lax.axis_index("grp")
    assert grp_count == 4

    owner_ids = owner_route[:, :, 0]
    hits = owner_ids[:, None, :] == jnp.arange(owners, dtype=jnp.int32)[None, :, None]
    earlier = jnp.arange(row_count)[:, None] < jnp.arange(row_count)[None, :]
    rank = mix(
        hits.reshape(STEPS * owners, row_count).astype(jnp.bfloat16), earlier.astype(jnp.bfloat16)
    )
    rank = jnp.sum(jnp.where(hits, rank.reshape(hits.shape), 0.0), axis=1).astype(jnp.int32)
    dest = owner_ids * capacity + rank
    dest_lanes = dest.reshape(STEPS, 1, row_count)

    places = jnp.arange(owners * capacity, dtype=jnp.int32)
    found = dest[:, None, :] == places[None, :, None]
    slots = jnp.sum(jnp.where(found, list_slot[:, None, :] + 1, 0), axis=2) - 1
    slots = slots.reshape(STEPS, owners, capacity).transpose(1, 0, 2)
    slots = exchange(slots.reshape(owners, 1, STEPS * capacity))

    first = pack_rows(vectors, dest_lanes, 0, owners, capacity, 1)
    first, slots = gate(first, slots)
    received0 = exchange(first)
    second = pack_rows(vectors, dest_lanes, 1, owners, capacity, 1)
    third = pack_rows(vectors, dest_lanes, 2, owners, capacity, 2)

    slots = slots.reshape(owners, STEPS, capacity).transpose(1, 0, 2)
    slots = slots.reshape(STEPS, owners * capacity)
    slot_cols = slots.T
    dest_cols = dest.T

    list_iota = jnp.arange(list_dev, dtype=jnp.int32)
    batch = jnp.sum((slots[:, None, :] == list_iota[None, :, None]).astype(jnp.int32), axis=2)
    batch = sum([batch] + [swap(batch, "grp", offset) for offset in range(1, grp_count)])
    weights = [counts]
    for step in range(STEPS):
        weights.append(weights[-1] + batch[step])
    weights = jnp.stack(weights).astype(jnp.float32).T

    high = group // 2
    low = (group ^ high) % 2
    places = jnp.stack([2 * low + high, 2 * high + low]).astype(jnp.int32)
    order = jnp.where(slots < list_dev // 2, places[0], places[1]) * (list_dev // 8)
    relative_slots = jnp.where(slots < 0, -1, slots ^ order).reshape(STEPS, 1, owners * capacity)

    def sums_of(rows, step):
        return list_sums(rows, 0, relative_slots, step, list_dev)

    def residual(rows, step, parts, into=None, place=0, count=1):
        return residual_rows(
            rows, 0, slot_cols, step, centroids, weights, parts, places, into, place, count
        )

    second, third, slot_cols, weights, received0 = gate(second, third, slot_cols, weights, received0)
    received1 = exchange(second)

    sums = sums_of(received0, 0)
    got = send_far(sums)
    buffer = residual(received0, 0, [], third, 1, 2)
    buffer, got = gate(buffer, got)
    done = send_near(sums, got)
    buffer, done, received1 = gate(buffer, done, received1)
    mixed = exchange(buffer)

    own = spread_near(done)
    received1, own = gate(received1, own)
    whole = spread_far(own)
    sums = sums_of(received1, 1)
    sums, whole = gate(sums, whole)
    parts = [whole]
    got = send_far(sums)
    buffer = residual(received1, 1, parts)
    buffer, got = gate(buffer, got)
    own = spread_near(send_near(sums, got))
    buffer, own, mixed = gate(buffer, own, mixed)
    back1 = exchange(buffer)

    parts = parts + [spread_far(own)]
    sums = sums_of(mixed, 2)
    got = send_far(sums)
    buffer = residual(mixed, 2, parts)
    output = unpack_rows(mixed, 1, dest_cols, 0, None, row_count)
    buffer, got, output, back1 = gate(buffer, got, output, back1)
    back2 = exchange(buffer)

    whole = spread_far(spread_near(send_near(sums, got)))
    current = new_rows(centroids, weights, parts + [whole], places, 0, None)
    output = unpack_rows(back1, 0, dest_cols, 1, output, row_count)
    output, current = gate(output, current)
    output = unpack_rows(back2, 0, dest_cols, 2, output, row_count)
    output, whole[1], whole[3] = gate(output, whole[1], whole[3])
    current = new_rows(centroids, weights, parts + [whole], places, 1, current)
    return (output, current)


def solution(mesh):
    in_specs = (
        P(None, ("grp", "list"), None),
        P(None, ("grp", "list"), None),
        P(None, ("grp", "list")),
        P("list", None),
        P("list"),
    )
    out_specs = (P(None, ("grp", "list"), None), P("list", None))
    return jax.shard_map(local, mesh=mesh, in_specs=in_specs, out_specs=out_specs, check_vma=False)
```
